32 devices in a mesh: clips: 2 (over y), ha: 4 (over z), wa: 2 (over core), ta: 2 (over x).
Axes of the slice: x: 2, y: 2, z: 4, core: 2. Of those that a mesh axis runs over, the one named last changes fastest.
Arguments:
- frames: bfloat16 [8, 16, 256, 128], P(('clips', 'ta'), 'ha', 'wa'), parts along dimension 0, may hold values from -12 to 12
- past_first: bfloat16 [4, 16, 256, 128], P('clips', 'ha', 'wa'), parts along dimension 0, may hold values from -6 to 6
- past_second: bfloat16 [4, 16, 256, 128], P('clips', 'ha', 'wa'), parts along dimension 0, may hold values from -6 to 6
- gain_first: float32 [128], replicated, may hold values from 0.5 to 1.5
- shift_first: float32 [128], replicated, may hold values from -3 to 3
- kernel_first: bfloat16 [3, 3, 3, 128, 128], replicated, may hold values from -0.109375 to 0.109375
- bias_first: float32 [128], replicated, may hold values from -2 to 2
- gain_second: float32 [128], replicated, may hold values from 0.5 to 1.5
- shift_second: float32 [128], replicated, may hold values from -3 to 3
- kernel_second: bfloat16 [3, 3, 3, 128, 128], replicated, may hold values from -0.109375 to 0.109375
- bias_second: float32 [128], replicated, may hold values from -2 to 2
Outputs:
- decoded: bfloat16 [8, 16, 256, 128], P(('clips', 'ta'), 'ha', 'wa'), parts along dimension 0
The draws below stay inside these ranges and needn't reach their ends.
There are 2 independent parts, one for each index of `clips`. The reference program is written for one: setup_inputs(seed, part) draws one part's arguments, and reference() takes and returns one part's arrays. A program takes and returns all parts, laid end to end along the dimension named above; an argument that names none is the same for every part. Nothing has to cross between parts.
All inputs are finite; a program needn't handle non-finite values.
Results may differ from the reference program's by a relative error of at most 0.0039.
Values may be sent and summed in bfloat16 or wider, within the bound.
No kernel may reach another device: no remote copies, remote signals or barrier semaphores. Data moves between devices by JAX's collectives and lax.ppermute only.
A program may use at most 64 MiB of HBM per device.

```python
import jax
import jax.numpy as jnp
from jax import lax

C = 128
G = 32
HB = 4
WB = 128
FRAMES = 4
H = 16
W = 256


def draw_frames(key, part):
    base = jax.random.fold_in(key, 11)
    key_noise = jax.random.fold_in(base, 0)
    key_rough = jax.random.fold_in(base, 1)
    key_band = jax.random.fold_in(base, 3)
    key_frame = jax.random.fold_in(base, 4)
    key_chan = jax.random.fold_in(base, 5)
    ramp = (jnp.arange(H, dtype=jnp.float32) / max(H - 1, 1)).reshape(1, H, 1, 1)
    time_ramp = (jnp.arange(FRAMES, dtype=jnp.float32) / max(FRAMES - 1, 1)).reshape(FRAMES, 1, 1, 1)
    band_index = (jnp.arange(W, dtype=jnp.int32) // WB).astype(jnp.float32)
    band_step = (band_index / max(W // WB - 1, 1)).reshape(1, 1, W, 1)
    rough = jax.random.uniform(key_rough, (FRAMES, H, W, 1), jnp.float32, 0.0, 1.0)
    height_log = jax.random.uniform(key_band, (H // HB,), jnp.float32, -1.0, 1.0)
    height_log = jnp.repeat(height_log, HB, total_repeat_length=H).reshape(1, H, 1, 1)
    frame_log = jax.random.uniform(key_frame, (FRAMES, 1, 1, 1), jnp.float32, -1.0, 1.0)
    chan_scale = jnp.exp(jax.random.uniform(key_chan, (1, 1, 1, C), jnp.float32, -0.7, 0.7))
    scale = 10.0 ** (0.5 * ramp + 0.4 * time_ramp + 0.4 * band_step + 0.5 * rough - 1.5)
    scale = scale * jnp.exp(height_log + frame_log)
    noise = jax.random.normal(key_noise, (FRAMES, H, W, C), jnp.float32)
    values = noise * chan_scale * scale
    return jnp.clip(values, -12.0, 12.0).astype(jnp.bfloat16)


def block_levels(key, extent, pieces, smallest, largest):
    def one(axis_at, shards_of):
        draws = jax.random.uniform(jax.random.fold_in(jax.random.fold_in(key, 6), axis_at), (shards_of,), jnp.float32, smallest / len(pieces), largest / len(pieces))
        return jnp.repeat(jnp.exp(draws), extent[axis_at] // shards_of).reshape((-1,) + (1,) * (len(extent) - axis_at - 1))

    factor_of = one(*pieces[0])
    for cut in pieces[1:]:
        factor_of = factor_of * one(*cut)
    return factor_of


def bell_draw(rng, dims, spread, most, shards=(), kind=jnp.bfloat16):
    drawn = spread * jax.random.normal(rng, dims, jnp.float32)
    if shards:
        drawn = drawn * block_levels(rng, dims, shards, -0.22, 0.18)
    return jnp.clip(drawn, -most, most).astype(kind)


def setup_inputs(seed: int = 0, part: int = 0) -> dict:
    splits = jax.random.split(jax.random.key(seed), 12)
    part_keys = jax.random.split(jax.random.fold_in(splits[11], part), 12)
    frames = draw_frames(jax.random.fold_in(jax.random.fold_in(splits[11], part), 71), part)
    past_first = bell_draw(part_keys[1], (2, H, W, C), 1.0, 6.0, ((1, 4), (2, 2)))
    past_second = bell_draw(part_keys[2], (2, H, W, C), 1.0, 6.0, ((1, 4), (2, 2)))
    gain_first = jnp.clip(jax.random.uniform(splits[3], (C,), jnp.float32, 0.5, 1.5), 0.5, 1.5)
    shift_first = bell_draw(splits[4], (C,), 0.5, 3.0, (), jnp.float32)
    kernel_first = bell_draw(splits[5], (3, 3, 3, C, C), (27 * C) ** -0.5, 0.109375)
    bias_first = bell_draw(splits[6], (C,), 0.3, 2.0, (), jnp.float32)
    gain_second = jnp.clip(jax.random.uniform(splits[7], (C,), jnp.float32, 0.5, 1.5), 0.5, 1.5)
    shift_second = bell_draw(splits[8], (C,), 0.5, 3.0, (), jnp.float32)
    kernel_second = bell_draw(splits[9], (3, 3, 3, C, C), (27 * C) ** -0.5, 0.109375)
    bias_second = bell_draw(splits[10], (C,), 0.3, 2.0, (), jnp.float32)
    return {"frames": frames, "past_first": past_first, "past_second": past_second, "gain_first": gain_first, "shift_first": shift_first, "kernel_first": kernel_first, "bias_first": bias_first, "gain_second": gain_second, "shift_second": shift_second, "kernel_second": kernel_second, "bias_second": bias_second}


EPS = 1e-06

def norm_silu(value, gain, shift):
    nframe, rows, cols, chans = value.shape
    grouped = value.reshape(nframe, rows, cols, G, chans // G)
    mean = lax.optimization_barrier(jnp.mean(grouped, axis=(0, 1, 2, 4)))
    square = lax.optimization_barrier(jnp.mean(grouped * grouped, axis=(0, 1, 2, 4)))
    inverse = lax.rsqrt(square - mean * mean + EPS)
    mean_chan = jnp.repeat(mean, chans // G)
    inverse_chan = jnp.repeat(inverse, chans // G)
    return jax.nn.silu((value - mean_chan) * inverse_chan * gain + shift)

def causal_conv(past, current, kernel, bias):
    joined = jnp.concatenate([past, current], axis=0)
    padded = jnp.pad(joined, ((0, 0), (1, 1), (1, 1), (0, 0)))
    nframe = current.shape[0]
    rows = current.shape[1]
    cols = current.shape[2]
    chans = current.shape[3]
    stacked = kernel.reshape(3, 3, 3 * chans, chans)
    outputs = []
    for frame in range(nframe):
        total = jnp.zeros((rows * cols, chans), jnp.float32) + bias
        for time_step in range(3):
            for row_step in range(3):
                slab = jnp.concatenate([padded[frame + time_step, row_step:row_step + rows, col_step:col_step + cols, :] for col_step in range(3)], axis=-1)
                total = total + jnp.dot(slab.reshape(rows * cols, 3 * chans), stacked[time_step, row_step], preferred_element_type=jnp.float32)
        outputs.append(total.reshape(rows, cols, chans))
    return jnp.stack(outputs, axis=0)

def reference(frames, past_first, past_second, gain_first, shift_first, kernel_first, bias_first, gain_second, shift_second, kernel_second, bias_second):
    source = frames.astype(jnp.float32)
    act_one = norm_silu(source, gain_first, shift_first).astype(jnp.bfloat16)
    hidden = causal_conv(past_first, act_one, kernel_first, bias_first)
    act_two = norm_silu(hidden, gain_second, shift_second).astype(jnp.bfloat16)
    result = causal_conv(past_second, act_two, kernel_second, bias_second) + source
    return result.astype(jnp.bfloat16)
```

```python
import jax
import jax.numpy as jnp
from jax import lax
from jax.sharding import PartitionSpec as P

G = 32


EPS = 1e-06


def shifted(value, axis, steps):
    count = lax.axis_size(axis)
    initial, last = (max(0, -steps), min(count, count - steps))
    return lax.ppermute(value, axis, [(source, source + steps) for source in range(initial, last)])


def extended(block, sides, width):
    for axis, dim in sides:
        count = lax.axis_size(axis)
        forward = [(i, i + 1) for i in range(count - 1)]
        backward = [(target, source) for source, target in forward]
        low = lax.ppermute(
            lax.slice_in_dim(block, block.shape[dim] - width, None, axis=dim), axis, forward
        )
        high = lax.ppermute(lax.slice_in_dim(block, 0, width, axis=dim), axis, backward)
        block = jnp.concatenate([low, block, high], axis=dim)
    return block


BANDS = ("ha", "wa", "ta")


def summed(parts):
    joined = jnp.concatenate(parts)
    count = lax.axis_size("ha") * lax.axis_size("wa") * lax.axis_size("ta")
    spread = jnp.broadcast_to(joined[None], (count, joined.shape[0]))
    gathered = lax.all_to_all(spread, BANDS, 0, 0, tiled=True)
    return jnp.split(jnp.sum(gathered, axis=0), len(parts))


def group_sums(value):
    nframe, rows, cols, chans = value.shape
    grouped = value.reshape(nframe, rows, cols, G, chans // G)
    return (jnp.sum(grouped, axis=(0, 1, 2, 4)), jnp.sum(grouped * grouped, axis=(0, 1, 2, 4)))


def apply_norm(value, totals, squares, count, gain, shift):
    chans = value.shape[3]
    mean = totals / count
    inverse = lax.rsqrt(squares / count - mean * mean + EPS)
    mean_chan = jnp.repeat(mean, chans // G)
    inverse_chan = jnp.repeat(inverse, chans // G)
    return jax.nn.silu((value - mean_chan) * inverse_chan * gain + shift)


def conv_block(padded, kernel, bias, nframe):
    out_rows = padded.shape[1] - 2
    out_cols = padded.shape[2] - 2
    chans = padded.shape[3]
    stacked = kernel.reshape(3, 3, 3 * chans, chans)
    total = jnp.zeros((nframe * out_rows * out_cols, chans), jnp.float32) + bias
    for time_step in range(3):
        for row_step in range(3):
            slab = jnp.concatenate(
                [
                    padded[
                        time_step : time_step + nframe,
                        row_step : row_step + out_rows,
                        col_step : col_step + out_cols,
                        :,
                    ]
                    for col_step in range(3)
                ],
                axis=3,
            )
            total = total + jnp.dot(
                slab.reshape(nframe * out_rows * out_cols, 3 * chans),
                stacked[time_step, row_step],
                preferred_element_type=jnp.float32,
            )
    return total.reshape(nframe, out_rows, out_cols, chans)


def on_device(
    frames,
    past_first,
    past_second,
    gain_first,
    shift_first,
    kernel_first,
    bias_first,
    gain_second,
    shift_second,
    kernel_second,
    bias_second,
):
    nframe, rows, cols, chans = frames.shape
    count = float(
        nframe
        * rows
        * cols
        * (chans // G)
        * lax.axis_size("ha")
        * lax.axis_size("wa")
        * lax.axis_size("ta")
    )
    source = frames.astype(jnp.float32)
    first_sum, first_square = group_sums(source)
    first_sum, first_square = summed((first_sum, first_square))
    act_one = apply_norm(source, first_sum, first_square, count, gain_first, shift_first).astype(
        jnp.bfloat16
    )
    first_time = lax.axis_index("ta") == 0
    carried = shifted(act_one, "ta", 1)
    carried = jnp.where(first_time, past_first, carried)
    joined = jnp.concatenate([carried, act_one], axis=0)
    padded = extended(joined, (("ha", 1), ("wa", 2)), 1)
    hidden = conv_block(padded, kernel_first, bias_first, nframe)
    second_sum, second_square = group_sums(hidden)
    second_sum, second_square = summed((second_sum, second_square))
    act_two = apply_norm(
        hidden, second_sum, second_square, count, gain_second, shift_second
    ).astype(jnp.bfloat16)
    carried_two = shifted(act_two, "ta", 1)
    carried_two = jnp.where(first_time, past_second, carried_two)
    joined_two = jnp.concatenate([carried_two, act_two], axis=0)
    padded_two = extended(joined_two, (("ha", 1), ("wa", 2)), 1)
    result = conv_block(padded_two, kernel_second, bias_second, nframe) + source
    return result.astype(jnp.bfloat16)


def solution(mesh):
    return jax.shard_map(
        on_device,
        mesh=mesh,
        in_specs=(
            P(("clips", "ta"), "ha", "wa", None),
            P("clips", "ha", "wa", None),
            P("clips", "ha", "wa", None),
            P(),
            P(),
            P(),
            P(),
            P(),
            P(),
            P(),
            P(),
        ),
        out_specs=P(("clips", "ta"), "ha", "wa", None),
        check_vma=False,
    )
```

```python
import functools

import jax
import jax.numpy as jnp
from jax import lax
from jax.experimental import pallas as pl
from jax.experimental.pallas import tpu as pltpu
from jax.sharding import PartitionSpec as P

G = 32
EPS = 1e-06
BANDS = ("ha", "wa", "ta")
VMEM = pl.BlockSpec(memory_space=pltpu.VMEM)
PAD = 8


def spread_sums(sums):
    count = lax.axis_size("ha") * lax.axis_size("wa") * lax.axis_size("ta")
    copies = jnp.broadcast_to(sums[None], (count, sums.shape[0]))
    return lax.all_to_all(copies, BANDS, 0, 0, tiled=True)


def across(value):
    return lax.ppermute(value, "wa", [(0, 1), (1, 0)])


def row_pairs(later):
    bands, times = lax.axis_size("ha"), lax.axis_size("ta")
    pairs = []
    for band in range(bands):
        for time in range(times - later):
            for core, target in ((0, band - 1), (1, band + 1)):
                if 0 <= target < bands:
                    pairs.append(
                        (
                            (band * 2 + core) * times + time,
                            (target * 2 + 1 - core) * times + time + later,
                        )
                    )
    return pairs


def group_total(value):
    lane = lax.broadcasted_iota(jnp.int32, value.shape, 1)
    chans = value.shape[1]
    pair = value + jnp.where(
        lane % 2 == 0, pltpu.roll(value, chans - 1, 1), pltpu.roll(value, 1, 1)
    )
    return pair + jnp.where(
        lane % 4 < 2, pltpu.roll(pair, chans - 2, 1), pltpu.roll(pair, 2, 1)
    )


def norm_terms(stats_ref, gain_ref, shift_ref, count):
    chans = gain_ref.shape[1]
    total = jnp.sum(stats_ref[...], axis=0, keepdims=True)
    both = jnp.concatenate([total[:, :chans], total[:, chans:]], axis=0)
    both = group_total(jnp.broadcast_to(both[:, None], (2, 8, chans)).reshape(16, chans))
    mean = both[:1] / count
    inverse = lax.rsqrt(both[8:9] / count - mean * mean + EPS)
    return mean, inverse * gain_ref[...] * 0.5, shift_ref[...] * 0.5


def activated(value, terms):
    mean, scale, shift = terms
    half = (value - mean) * scale + shift
    return half + half * jnp.tanh(half)


def pair_weights(w_ref, pair_ref):
    depth, chans = w_ref.shape[1:]
    for tap in range(3):
        for row in range(4):
            for side in range(2):
                at = pair_ref.at[tap * 4 + row, :, pl.ds(side * chans, chans)]
                if 0 <= row - side < 3:
                    at[...] = w_ref[tap * 3 + row - side]
                else:
                    at[...] = jnp.zeros((depth, chans), w_ref.dtype)


def put_row(slab_ref, stage_ref, slot, row, frame):
    cols, chans = slab_ref.shape[2], slab_ref.shape[3] // 3
    for tap in range(3):
        slab_ref[row, frame, :, tap * chans : (tap + 1) * chans] = stage_ref[
            slot, PAD - 1 + tap : PAD - 1 + tap + cols, :
        ].astype(jnp.bfloat16)


def put_halves(slab_ref, stage_ref, slot, core, row, frame, mine, other):
    half = mine.shape[0]
    stage_ref[slot, pl.ds(pl.multiple_of(PAD + core * half, PAD), half), :] = mine
    stage_ref[slot, pl.ds(pl.multiple_of(PAD + (1 - core) * half, PAD), half), :] = other
    put_row(slab_ref, stage_ref, slot, row, frame)


def clear_row(slab_ref, row, frame):
    slab_ref[row, frame] = jnp.zeros(slab_ref.shape[2:], slab_ref.dtype)


def outside(core):
    band = lax.axis_index("ha")
    return band == (lax.axis_size("ha") - 1) * core


def put_block(slab_ref, stage_ref, core, first, mine_ref, other_ref, edge_ref, at, apply):
    for frame in range(2):
        for inner in range(3):
            put_halves(
                slab_ref, stage_ref, (frame * 3 + inner) % 2, core, inner + 1 - core, first + frame,
                apply(mine_ref[frame, inner + core].astype(jnp.float32)),
                apply(other_ref[frame, inner + core].astype(jnp.float32)),
            )
        put_halves(
            slab_ref, stage_ref, frame % 2, core, 3 * core, first + frame,
            apply(edge_ref[at + 2 + frame].astype(jnp.float32)),
            apply(edge_ref[at + frame].astype(jnp.float32)),
        )


def convolve(slab_ref, pair_ref, acc_ref, nout):
    cols, chans = slab_ref.shape[2], slab_ref.shape[3] // 3
    for tap in range(3):
        for row in range(4):
            part = jnp.dot(
                slab_ref[row, tap : tap + nout].reshape(nout * cols, 3 * chans),
                pair_ref[tap * 4 + row],
                preferred_element_type=jnp.float32,
            )
            if tap == 0 and row == 0:
                acc_ref[...] = part
            else:
                acc_ref[...] += part


def clear_pads(stage_ref):
    depth = stage_ref.shape[1]
    for slot in range(stage_ref.shape[0]):
        for start in (0, depth - PAD):
            stage_ref[slot, start : start + PAD, :] = jnp.zeros(
                (PAD, stage_ref.shape[2]), stage_ref.dtype
            )


def first_kernel(count, far, *refs):
    (stats_ref, gain_ref, shift_ref, bias_ref, w_ref, fm, fo, cm, co, pm, po, edge, cedge, *rest) = refs
    if far:
        dm, do, dedge, *rest = rest
    outer_ref, inner_ref, sums_ref, slab_ref, stage_ref, pair_ref, acc_ref = rest
    core, time = lax.axis_index("wa"), lax.axis_index("ta")
    chans = gain_ref.shape[1]
    cols = slab_ref.shape[2]
    pair_weights(w_ref, pair_ref)
    clear_pads(stage_ref)
    terms = norm_terms(stats_ref, gain_ref, shift_ref, count)
    act = functools.partial(activated, terms=terms)
    put = functools.partial(put_block, slab_ref, stage_ref, core)
    put(4, fm, fo, edge, 0, act)

    @pl.when(time == 0)
    def _():
        put(2, pm, po, edge, 4, lambda value: value)

    @pl.when(time > 0)
    def _():
        put(2, cm, co, cedge, 0, act)

    if far:

        @pl.when(time > 1)
        def _():
            put(0, dm, do, dedge, 0, act)

    @pl.when(time <= 1)
    def _():
        put(0, pm, po, edge, 4, lambda value: value)

    @pl.when(outside(core))
    def _():
        for frame in range(6):
            clear_row(slab_ref, 3 * core, frame)

    convolve(slab_ref, pair_ref, acc_ref, 4)
    for row, ref_of in ((0, None), (1, None)):
        value = acc_ref[:, row * chans : (row + 1) * chans] + bias_ref[...]
        own = value[2 * cols :]
        total = jnp.sum(own, axis=0, keepdims=True)
        square = jnp.sum(own * own, axis=0, keepdims=True)
        if row == 0:
            sums_ref[:, :chans] = total
            sums_ref[:, chans:] = square
        else:
            sums_ref[:, :chans] += total
            sums_ref[:, chans:] += square

        @pl.when(core == row)
        def _():
            outer_ref[...] = value.reshape(4, cols, chans)

        @pl.when(core != row)
        def _():
            inner_ref[...] = value.reshape(4, cols, chans)


def second_kernel(count, *refs):
    (stats_ref, gain_ref, shift_ref, bias_ref, w_ref, beyond, outer, inner, near, pm, po, edge, fm, fo) = refs[:14]
    keep_ref, send_ref, slab_ref, stage_ref, pair_ref, acc_ref = refs[14:]
    core, time = lax.axis_index("wa"), lax.axis_index("ta")
    chans = gain_ref.shape[1]
    cols = slab_ref.shape[2]
    half = cols // 2
    pair_weights(w_ref, pair_ref)
    clear_pads(stage_ref)
    terms = norm_terms(stats_ref, gain_ref, shift_ref, count)

    def put_hidden(frame):
        for place, ref in enumerate((beyond, outer, inner, near)):
            slot = place % 2
            stage_ref[slot, PAD : PAD + cols, :] = activated(ref[frame], terms)
            put_row(slab_ref, stage_ref, slot, place + core * (3 - 2 * place), frame)

    put_hidden(2)
    put_hidden(3)

    @pl.when(time == 0)
    def _():
        put_block(slab_ref, stage_ref, core, 0, pm, po, edge, 8, lambda value: value)

    @pl.when(time > 0)
    def _():
        put_hidden(0)
        put_hidden(1)

    @pl.when(outside(core))
    def _():
        for frame in range(4):
            clear_row(slab_ref, 3 * core, frame)

    convolve(slab_ref, pair_ref, acc_ref, 2)
    for frame in range(2):
        for row in range(2):
            for ref, source, side in ((keep_ref, fm, core), (send_ref, fo, 1 - core)):
                start = pl.multiple_of(frame * cols + side * half, half)
                value = acc_ref[pl.ds(start, half), row * chans : (row + 1) * chans] + bias_ref[...]
                value = value + source[frame, row + 2 * core].astype(jnp.float32)
                ref[frame, row] = value.astype(ref.dtype)


def scratch(frames, nout, cols, chans):
    return [
        pltpu.VMEM((4, frames, cols, 3 * chans), jnp.bfloat16),
        pltpu.VMEM((2, cols + 2 * PAD, chans), jnp.float32),
        pltpu.VMEM((12, 3 * chans, 2 * chans), jnp.bfloat16),
        pltpu.VMEM((nout * cols, 2 * chans), jnp.float32),
    ]


def on_device(
    frames,
    past_first,
    past_second,
    gain_first,
    shift_first,
    kernel_first,
    bias_first,
    gain_second,
    shift_second,
    kernel_second,
    bias_second,
):
    nframe, rows, half, chans = frames.shape
    bands, cores, times = (lax.axis_size(axis) for axis in BANDS)
    assert (nframe, rows, cores) == (2, 4, 2)
    cols = 2 * half
    count = float(nframe * rows * half * (chans // G) * bands * cores * times)
    core = lax.axis_index("wa")
    far = times > 2

    def later(value, steps):
        return lax.ppermute(value, "ta", [(i, i + steps) for i in range(times - steps)])

    def flat(vector):
        return vector.reshape(1, -1)

    def stacked(kernel):
        return kernel.reshape(9, 3 * chans, chans)

    carried = later(frames, 1)
    frames_over, first_over, second_over = across(frames), across(past_first), across(past_second)
    outer = jnp.concatenate(
        [
            lax.dynamic_slice_in_dim(value, (rows - 1) * core, 1, 1)[:, 0]
            for value in (frames, frames_over, past_first, first_over, past_second, second_over)
        ]
    )
    edge = lax.ppermute(outer, BANDS, row_pairs(0))
    carried_edge = lax.ppermute(outer[:4], BANDS, row_pairs(1))
    source = frames.astype(jnp.float32)
    sums = jnp.concatenate(
        [jnp.sum(source, axis=(0, 1, 2)), jnp.sum(source * source, axis=(0, 1, 2))]
    )
    gathered = spread_sums(sums)
    behind = [carried, across(carried)]
    operands = [frames, frames_over, *behind, past_first, first_over, edge, carried_edge]
    if far:
        distant = later(frames, 2)
        operands += [distant, across(distant), lax.ppermute(outer[:4], BANDS, row_pairs(2))]
    hidden_row = jax.ShapeDtypeStruct((4, cols, chans), jnp.float32)
    outer_row, inner_row, sums = pl.pallas_call(
        functools.partial(first_kernel, count, far),
        out_shape=(hidden_row, hidden_row, jax.ShapeDtypeStruct((1, 2 * chans), jnp.float32)),
        in_specs=[VMEM] * (5 + len(operands)),
        out_specs=[VMEM] * 3,
        scratch_shapes=scratch(6, 4, cols, chans),
        name="first_conv",
    )(gathered, flat(gain_first), flat(shift_first), flat(bias_first), stacked(kernel_first), *operands)
    beyond_row = lax.ppermute(outer_row, BANDS, row_pairs(0))
    near_row = across(inner_row)
    gathered = spread_sums(sums[0])
    band_half = jax.ShapeDtypeStruct((nframe, 2, half, chans), jnp.bfloat16)
    keep, send = pl.pallas_call(
        functools.partial(second_kernel, count),
        out_shape=(band_half, band_half),
        in_specs=[VMEM] * 14,
        out_specs=[VMEM] * 2,
        scratch_shapes=scratch(4, 2, cols, chans),
        name="second_conv",
    )(
        gathered,
        flat(gain_second),
        flat(shift_second),
        flat(bias_second),
        stacked(kernel_second),
        beyond_row,
        outer_row,
        inner_row,
        near_row,
        past_second,
        second_over,
        edge,
        frames,
        frames_over,
    )
    got = across(send)
    return jnp.where(
        core == 0, jnp.concatenate([keep, got], axis=1), jnp.concatenate([got, keep], axis=1)
    )


def solution(mesh):
    bands = P(("clips", "ta"), "ha", "wa", None)
    past = P("clips", "ha", "wa", None)
    return jax.shard_map(
        on_device,
        mesh=mesh,
        in_specs=(bands, past, past) + (P(),) * 8,
        out_specs=bands,
        check_vma=False,
    )
```
